128 devices in a mesh: section: 4 (over z_lo, core), dp: 16 (over y, x), tensor: 2 (over z_hi).
Axes of the slice: x: 4, y: 4, z: 4 (z_hi: 2, z_lo: 2; z = z_hi * 2 + z_lo), core: 2. Of those that a mesh axis runs over, the one named last changes fastest.
Arguments:
- grad_hidden: bfloat16 [4, 2048, 16384], P('section', None, ('dp', 'tensor')), may hold values from -6 to 6
- gate_pre: bfloat16 [4, 2048, 16384], P('section', None, ('dp', 'tensor')), may hold values from -6 to 6
- up_pre: bfloat16 [4, 2048, 16384], P('section', None, ('dp', 'tensor')), may hold values from -6 to 6
- w_gate: bfloat16 [4, 16384, 6144], P('section', ('dp', 'tensor')), may hold values from -0.078125 to 0.078125
- w_up: bfloat16 [4, 16384, 6144], P('section', ('dp', 'tensor')), may hold values from -0.078125 to 0.078125
- block_expert: int32 [4, 16], P('section'), may hold values from 0 to 1
Outputs:
- prev_grad: bfloat16 [4, 2048, 6144], P('section', ('dp', 'tensor'))
The draws below stay inside these ranges and needn't reach their ends.
Inputs may be any that keep to these rules, and one draw needn't show every extreme that they name: block_expert[s, b] is the expert of rows b * 128 to (b + 1) * 128 - 1 of layer s.
All inputs are finite; a program needn't handle non-finite values.
Results may differ from the reference program's by a relative error of at most 0.019.
Values may be sent and summed in bfloat16 or wider, within the bound.
A program may use at most 192 MiB of HBM per device.

```python
import math
import jax
import jax.numpy as jnp
import numpy as np
from jax import lax

D = 6144
F = 8192
EXPERTS = 2
BLOCK = 128
SECTIONS = 4
BLOCKS = 16
ROWS = 2048
HID_DEV = 512


def touch_ends(values, key, smallest, top_value):
    index_at = [jax.random.randint(jax.random.fold_in(key, axis), (), 0, length) for axis, length in enumerate(values.shape)]
    main_axis = values.shape.index(max(values.shape))
    neighbour = index_at[:main_axis] + [(index_at[main_axis] + 1) % values.shape[main_axis]] + index_at[main_axis + 1:]
    return values.at[tuple(index_at)].set(smallest).at[tuple(neighbour)].set(top_value)


def with_spikes(entries, rng, source, target, parts, factor):
    owner, partner = [(jnp.arange(entries.shape[axis_at]) // (entries.shape[axis_at] // parts)).reshape([-1 if axis == axis_at else 1 for axis in range(entries.ndim)]) for axis_at in (source, target)]
    chosen = jax.random.permutation(rng, parts)[partner]
    strong = (owner == chosen) | (owner == (partner + parts // 2) % parts)
    return jnp.where(strong, factor * entries, entries)


def level_of(key, shape, split, low, largest):
    def one(position, shards_of):
        steps = jax.random.uniform(jax.random.fold_in(jax.random.fold_in(key, 6), position), (shards_of,), jnp.float32, low / len(split), largest / len(split))
        return jnp.repeat(jnp.exp(steps), shape[position] // shards_of).reshape((-1,) + (1,) * (len(shape) - position - 1))

    loudness = one(*split[0])
    for cut in split[1:]:
        loudness = loudness * one(*cut)
    return loudness


def rank_table(amount, skew):
    weights = [(1 << 20) // math.isqrt(grade ** skew) + 1 for grade in range(1, amount + 1)]
    deviation = 1 + sum(weights) // (1 << 30)
    return np.cumsum(np.array([max(1, weight // deviation) for weight in weights]))


def skewed_ids(rng, extent, number_of, slope):
    listing = rank_table(number_of, slope)
    pick = jax.random.randint(jax.random.fold_in(rng, 1), extent, 0, int(listing[number_of - 1]))
    grade = jnp.searchsorted(jnp.asarray(listing, jnp.int32), pick, side="right")
    return jax.random.permutation(jax.random.fold_in(rng, 2), number_of)[grade].astype(jnp.int32)


def gaussian(key, shape, deviation, most, pieces=(), held_as=jnp.bfloat16):
    values = deviation * jax.random.normal(key, shape, jnp.float32)
    if pieces:
        values = values * level_of(key, shape, pieces, -0.22, 0.18)
    return jnp.clip(values, -most, most).astype(held_as)


def heavy_noise(stream_key, shape, deviation, bound, cuts, heavy, kind=jnp.bfloat16):
    drawn = deviation * jax.random.normal(stream_key, shape, jnp.float32)
    if cuts:
        drawn = drawn * level_of(stream_key, shape, cuts, -0.22, 0.18)
    return jnp.clip(with_spikes(drawn, jax.random.fold_in(stream_key, 3), *heavy), -bound, bound).astype(kind)


def setup_inputs(seed: int = 0) -> dict:
    seeds = jax.random.split(jax.random.key(seed), 7)
    grad_hidden = heavy_noise(seeds[0], (SECTIONS, ROWS, EXPERTS * F), 1.0, 6.0, ((0, 4), (2, 32)), (2, 1, 32, 2.75))
    gate_pre = gaussian(seeds[1], (SECTIONS, ROWS, EXPERTS * F), 1.0, 6.0, ((0, 4), (2, 32)))
    up_pre = gaussian(seeds[2], (SECTIONS, ROWS, EXPERTS * F), 1.0, 6.0, ((0, 4), (2, 32)))
    w_gate = gaussian(seeds[3], (SECTIONS, EXPERTS * F, D), D ** -0.5, 0.078125, ((0, 4), (1, 32)))
    w_up = gaussian(seeds[4], (SECTIONS, EXPERTS * F, D), D ** -0.5, 0.078125, ((0, 4), (1, 32)))
    block_expert = touch_ends(skewed_ids(seeds[5], (SECTIONS, BLOCKS), EXPERTS, 2), jax.random.fold_in(seeds[5], 3), 0, EXPERTS - 1).astype(jnp.int32)
    return dict(grad_hidden=grad_hidden, gate_pre=gate_pre, up_pre=up_pre, w_gate=w_gate, w_up=w_up, block_expert=block_expert)


def reference(grad_hidden, gate_pre, up_pre, w_gate, w_up, block_expert):
    groups = F // HID_DEV

    def one_section(items):
        grad_all, gate_all, up_all, gate_weight, up_weight, layout = items

        def one_block(block_id):
            expert_id = layout[block_id]
            first_row = (block_id * BLOCK).astype(jnp.int32)
            first_col = (expert_id * F).astype(jnp.int32)
            grad_rows = lax.dynamic_slice_in_dim(lax.dynamic_slice_in_dim(grad_all, first_row, BLOCK, 0), first_col, F, 1)
            gate_rows = lax.dynamic_slice_in_dim(lax.dynamic_slice_in_dim(gate_all, first_row, BLOCK, 0), first_col, F, 1)
            up_rows = lax.dynamic_slice_in_dim(lax.dynamic_slice_in_dim(up_all, first_row, BLOCK, 0), first_col, F, 1)
            gate_mat = lax.dynamic_slice_in_dim(gate_weight, first_col, F, 0)
            up_mat = lax.dynamic_slice_in_dim(up_weight, first_col, F, 0)
            gate_f = gate_rows.astype(jnp.float32)
            sig_gate = jax.nn.sigmoid(gate_f)
            grad_f = grad_rows.astype(jnp.float32)
            grad_gate = (grad_f * up_rows.astype(jnp.float32) * sig_gate * (1.0 + gate_f * (1.0 - sig_gate))).astype(jnp.bfloat16)
            grad_up = (grad_f * gate_f * sig_gate).astype(jnp.bfloat16)
            gate_groups = grad_gate.astype(jnp.float32).reshape(BLOCK, groups, HID_DEV)
            up_groups = grad_up.astype(jnp.float32).reshape(BLOCK, groups, HID_DEV)
            gate_split = gate_mat.astype(jnp.float32).reshape(groups, HID_DEV, D)
            up_split = up_mat.astype(jnp.float32).reshape(groups, HID_DEV, D)
            terms = jnp.einsum('rpi,pid->prd', gate_groups, gate_split) + jnp.einsum('rpi,pid->prd', up_groups, up_split)
            rounded = lax.optimization_barrier(terms.astype(jnp.bfloat16)).astype(jnp.float32)
            return jnp.sum(rounded, axis=0).astype(jnp.bfloat16)

        blocks_out = lax.map(one_block, jnp.arange(BLOCKS, dtype=jnp.int32))
        return blocks_out.reshape(ROWS, D)

    input_grad = lax.map(one_section, (grad_hidden, gate_pre, up_pre, w_gate, w_up, block_expert))
    return jnp.roll(input_grad, -1, axis=0)
```

```python
import jax
import jax.numpy as jnp
from jax import lax
from jax.experimental import pallas as pl
from jax.experimental.pallas import tpu as pltpu
from jax.sharding import PartitionSpec as P

F = 8192
BLOCK = 128
RING = 4
HALF = BLOCK // 2
CHUNKS = 4
TILE = 256
MESH = pl.DeviceIdType.MESH


def swiglu_grads(grad_rows, gate_rows, up_rows):
    gate_f = gate_rows.astype(jnp.float32)
    sig_gate = jax.nn.sigmoid(gate_f)
    grad_f = grad_rows.astype(jnp.float32)
    grad_gate = grad_f * up_rows.astype(jnp.float32) * sig_gate * (1.0 + gate_f * (1.0 - sig_gate))
    grad_up = grad_f * gate_f * sig_gate
    return grad_gate.astype(jnp.bfloat16), grad_up.astype(jnp.bfloat16)


def kernel(
    acts_hbm, gate_hbm, up_hbm, out_ref,
    acts, weights, first, second, third, near, far, last,
    acts_sem, load_sem, send1, recv1, send2, recv2, send3, recv3, send4, recv4, send5, recv5,
):
    section = lax.axis_index("section")
    dp = lax.axis_index("dp")
    tensor = lax.axis_index("tensor")
    y, x = dp // RING, dp % RING
    hidden = gate_hbm.shape[0]
    width = weights.shape[3]
    part_width = CHUNKS * width

    def turned(value, by):
        return (value + by) % RING

    def at_x(by):
        return (section, y * RING + turned(x, by), tensor)

    def at_y(by):
        return (section, turned(y, by) * RING + x, tensor)

    outer = (x, y)
    inner = (y, x)
    outer_device = (at_x, at_y)
    inner_device = (at_y, at_x)
    before = (section + 3) % 4
    after = (section + 1) % 4

    def load(part, c, kind):
        source = (gate_hbm, up_hbm)[kind]
        columns = pl.ds(pl.multiple_of(part * part_width + c * width, 128), width)
        return pltpu.make_async_copy(
            source.at[:, columns],
            weights.at[part, c, pl.ds(kind * hidden, hidden), :],
            load_sem.at[part, c, kind],
        )

    acts_copy = pltpu.make_async_copy(acts_hbm, acts, acts_sem)
    acts_copy.start()

    @pl.loop(0, CHUNKS)
    def _(c):
        for part in range(2):
            for kind in range(2):
                load(part, c, kind).start()

    barrier = pltpu.get_barrier_semaphore()
    peers = [at_x(1), at_x(3), at_y(1), at_y(3)]
    peers += [(s, dp, t) for s in (before, after) for t in range(2)]
    for peer in peers:
        pl.semaphore_signal(barrier, inc=1, device_id=peer, device_id_type=MESH)
    pl.semaphore_wait(barrier, len(peers))

    def remote(src, dst, send, recv, device):
        return pltpu.make_async_remote_copy(
            src_ref=src, dst_ref=dst, send_sem=send, recv_sem=recv, device_id=device, device_id_type=MESH
        )

    def step1(part, c, way):
        return remote(
            first.at[part, c, way], second.at[part, c, way, way],
            send1.at[part, c, way], recv1.at[part, c, way], outer_device[part](1 if way == 0 else 3),
        )

    def step2(part, c, way):
        return remote(
            second.at[part, c, way], third.at[part, c, way],
            send2.at[part, c, way], recv2.at[part, c, way], outer_device[part](1 if way == 0 else 3),
        )

    def step3(part, c, way):
        return remote(
            third.at[part, c, 0, way, turned(inner[part], 2)], near.at[part, c, way],
            send3.at[part, c, way], recv3.at[part, c, way], inner_device[part](1 if way == 0 else 3),
        )

    def step4(part, c, way):
        by = 1 if way == 0 else 3
        return remote(
            third.at[part, c, 0, :, turned(inner[part], by)], far.at[part, c, way],
            send4.at[part, c, way], recv4.at[part, c, way], inner_device[part](by),
        )

    def step5(part, c, half):
        return remote(
            third.at[part, c, 0, half, inner[part]], last.at[part, c, tensor],
            send5.at[part, c, half], recv5.at[part, c, tensor], (before, dp, half),
        )

    def step5_in(part, c, source):
        return remote(
            third.at[part, c, 0, 0, inner[part]], last.at[part, c, source],
            send5.at[part, c, 0], recv5.at[part, c, source], (before, dp, 0),
        )

    def product(part, c, chunk, j):
        rows = acts[:, chunk] if part == 0 else acts[chunk]
        rows = rows.reshape(RING * BLOCK, 2 * hidden)
        columns = pl.ds(pl.multiple_of(j * TILE, TILE), TILE)
        total = jnp.dot(rows, weights[part, c, :, columns], preferred_element_type=jnp.float32)
        return total.reshape(RING, 2, HALF, TILE), columns

    acts_copy.wait()

    @pl.loop(0, CHUNKS)
    def _(c):
        for part in range(2):
            for kind in range(2):
                load(part, c, kind).wait()

            @pl.loop(0, width // TILE)
            def _(j):
                total, columns = product(part, c, turned(outer[part], 2), j)
                for way in range(2):
                    first[part, c, way, :, :, columns] = total[:, way].astype(jnp.bfloat16)

            for way in range(2):
                step1(part, c, way).start()

    @pl.loop(0, CHUNKS)
    def _(c):
        for part in range(2):
            for way in range(2):
                step1(part, c, way).wait_recv()

                @pl.loop(0, width // TILE)
                def _(j):
                    total, columns = product(part, c, turned(outer[part], 1 if way == 0 else 3), j)
                    held = second[part, c, way, way, :, :, columns].astype(jnp.float32)
                    second[part, c, way, way, :, :, columns] = (total[:, way] + held).astype(jnp.bfloat16)
                    second[part, c, way, 1 - way, :, :, columns] = total[:, 1 - way].astype(jnp.bfloat16)

                step2(part, c, way).start()

    @pl.loop(0, CHUNKS)
    def _(c):
        for part in range(2):
            for way in range(2):
                step2(part, c, way).wait_recv()

            @pl.loop(0, width // TILE)
            def _(j):
                total, columns = product(part, c, outer[part], j)
                for half in range(2):
                    held = third[part, c, 0, half, :, :, columns].astype(jnp.float32)
                    held += third[part, c, 1, half, :, :, columns].astype(jnp.float32)
                    third[part, c, 0, half, :, :, columns] = (total[:, half] + held).astype(jnp.bfloat16)

            for way in range(2):
                step3(part, c, way).start()

    @pl.loop(0, CHUNKS)
    def _(c):
        for part in range(2):
            for way in range(2):
                step3(part, c, way).wait_recv()
                spot = turned(inner[part], 1 if way == 0 else 3)
                total = third[part, c, 0, way, spot].astype(jnp.float32)
                total += near[part, c, way].astype(jnp.float32)
                third[part, c, 0, way, spot] = total.astype(jnp.bfloat16)
                step4(part, c, way).start()

    @pl.loop(0, CHUNKS)
    def _(c):
        for part in range(2):
            for way in range(2):
                step4(part, c, way).wait_recv()
            for half in range(2):
                total = third[part, c, 0, half, inner[part]].astype(jnp.float32)
                total += far[part, c, 0, half].astype(jnp.float32)
                total += far[part, c, 1, half].astype(jnp.float32)
                third[part, c, 0, half, inner[part]] = total.astype(jnp.bfloat16)
                step5(part, c, half).start()

    @pl.loop(0, CHUNKS)
    def _(c):
        for part in range(2):
            for source in range(2):
                step5_in(part, c, source).wait_recv()
            total = last[part, c, 0].astype(jnp.float32) + last[part, c, 1].astype(jnp.float32)
            columns = pl.ds(pl.multiple_of(part * part_width + c * width, 128), width)
            out_ref[:, columns] = total.astype(jnp.bfloat16)

    @pl.loop(0, CHUNKS)
    def _(c):
        for part in range(2):
            for way in range(2):
                for step in (step1, step2, step3, step4, step5):
                    step(part, c, way).wait_send()


def per_device(grad_hidden, gate_pre, up_pre, w_gate, w_up, block_expert):
    hidden, model = w_gate.shape[1:]
    rows = grad_hidden.shape[1]
    width = model // 2 // CHUNKS
    my_expert = (lax.axis_index("dp") * lax.axis_size("tensor") + lax.axis_index("tensor")) * hidden // F
    mine = jnp.repeat(block_expert[0] == my_expert, BLOCK)[:, None]
    pair = swiglu_grads(grad_hidden[0], gate_pre[0], up_pre[0])
    acts = jnp.where(mine, jnp.concatenate(pair, axis=1), jnp.zeros((), jnp.bfloat16))
    acts = acts.reshape(RING, RING, BLOCK, 2 * hidden)
    bf16 = jnp.bfloat16
    dma = pltpu.SemaphoreType.DMA
    out = pl.pallas_call(
        kernel,
        out_shape=jax.ShapeDtypeStruct((HALF, model), bf16),
        in_specs=[pl.BlockSpec(memory_space=pl.ANY)] * 3,
        out_specs=pl.BlockSpec(memory_space=pltpu.VMEM),
        scratch_shapes=[
            pltpu.VMEM((RING, RING, BLOCK, 2 * hidden), bf16),
            pltpu.VMEM((2, CHUNKS, 2 * hidden, width), bf16),
            pltpu.VMEM((2, CHUNKS, 2, RING, HALF, width), bf16),
            pltpu.VMEM((2, CHUNKS, 2, 2, RING, HALF, width), bf16),
            pltpu.VMEM((2, CHUNKS, 2, 2, RING, HALF, width), bf16),
            pltpu.VMEM((2, CHUNKS, 2, HALF, width), bf16),
            pltpu.VMEM((2, CHUNKS, 2, 2, HALF, width), bf16),
            pltpu.VMEM((2, CHUNKS, 2, HALF, width), bf16),
            dma,
            dma((2, CHUNKS, 2)),
        ]
        + [dma((2, CHUNKS, 2))] * 10,
        cost_estimate=pl.CostEstimate(
            flops=4 * rows * hidden * model, bytes_accessed=4 * hidden * (rows + model), transcendentals=0
        ),
        compiler_params=pltpu.CompilerParams(
            collective_id=0, has_side_effects=True, vmem_limit_bytes=60 * 1024 * 1024
        ),
    )(acts, w_gate[0], w_up[0])
    return out[None]


def solution(mesh):
    return jax.shard_map(
        per_device,
        mesh=mesh,
        in_specs=(
            P("section", None, ("dp", "tensor")),
            P("section", None, ("dp", "tensor")),
            P("section", None, ("dp", "tensor")),
            P("section", ("dp", "tensor"), None),
            P("section", ("dp", "tensor"), None),
            P("section", None),
        ),
        out_specs=P("section", ("dp", "tensor"), None),
        check_vma=False,
    )
```

```python
import jax
import jax.numpy as jnp
from jax import lax
from jax.experimental import pallas as pl
from jax.experimental.pallas import tpu as pltpu
from jax.sharding import PartitionSpec as P

F = 8192
BLOCK = 128
RING = 4
HALF = BLOCK // 2
QUARTER = HALF // 2
CHUNKS = 5
WIDE = 2
R_CHUNKS = 2
LAGS = (0, 2, 3, 6, 7, 8)
R_LAGS = (0, 3, 5, 6, 11, 12)
TILE = 256
MESH = pl.DeviceIdType.MESH


def swiglu_grads(grad_rows, gate_rows, up_rows, mine):
    gate_f = gate_rows.astype(jnp.float32)
    sig_gate = jax.nn.sigmoid(gate_f)
    grad_f = jnp.where(mine, grad_rows.astype(jnp.float32), 0.0)
    grad_gate = grad_f * up_rows.astype(jnp.float32) * sig_gate * (1.0 + gate_f * (1.0 - sig_gate))
    grad_up = grad_f * gate_f * sig_gate
    return grad_gate.astype(jnp.bfloat16), grad_up.astype(jnp.bfloat16)


def kernel(
    layout_ref, grad_hbm, gate_hbm, up_hbm, w_gate_hbm, w_up_hbm, out_hbm,
    stage, acts, weights,
    first, second, third, across, near, far,
    halved, joined, r_first, r_second, r_third, r_near, r_far,
    stage_sem, load_sem,
    send1, recv1, send2, recv2, send3, recv3, send4, recv4, send5, recv5, send6, recv6,
    r_send0, r_recv0, r_send1, r_recv1, r_send2, r_recv2, r_send4, r_recv4, r_send5, r_recv5, r_send6, r_recv6,
):
    section = lax.axis_index("section")
    dp = lax.axis_index("dp")
    tensor = lax.axis_index("tensor")
    y, x = dp // RING, dp % RING
    hidden = w_gate_hbm.shape[0]
    width = WIDE * TILE
    my_expert = (dp * 2 + tensor) * hidden // F

    def turned(value, by):
        return (value + by) % RING

    def at_x(by):
        return (section, y * RING + turned(x, by), tensor)

    def at_y(by):
        return (section, turned(y, by) * RING + x, tensor)

    outer = (x, y)
    inner = (y, x)
    outer_device = (at_x, at_y)
    inner_device = (at_y, at_x)
    partner = (section, dp, 1 - tensor)
    before = ((section + 3) % 4, dp, tensor)
    after = ((section + 1) % 4, dp, tensor)
    order = (2, 1, 3, 0)

    def fetch(k, kind):
        source = (grad_hbm, gate_hbm, up_hbm)[kind]
        return pltpu.make_async_copy(source.at[:, turned(x, order[k])], stage.at[k % 2, kind], stage_sem.at[k, kind])

    def tile_of(part, c, j):
        return (part * CHUNKS + c) * WIDE + j

    def r_tile_of(part, c):
        return 2 * CHUNKS * WIDE + part * R_CHUNKS + c

    def columns_of(tile, count):
        return pl.ds(pl.multiple_of(tile * TILE, TILE), count * TILE)

    def load(tile, kind):
        source = (w_gate_hbm, w_up_hbm)[kind]
        return pltpu.make_async_copy(
            source.at[:, columns_of(tile, 1)],
            weights.at[tile, pl.ds(kind * hidden, hidden), :],
            load_sem.at[tile, kind],
        )

    def load_start(tile):
        for kind in range(2):
            load(tile, kind).start()

    def load_wait(tile):
        for kind in range(2):
            load(tile, kind).wait()

    for kind in range(3):
        fetch(0, kind).start()
    for j in range(WIDE):
        load_start(tile_of(0, 0, j))
    for kind in range(3):
        fetch(1, kind).start()
    for j in range(WIDE):
        load_start(tile_of(1, 0, j))

    @pl.loop(0, R_CHUNKS)
    def _(c):
        for part in range(2):
            load_start(r_tile_of(part, c))

    @pl.loop(1, CHUNKS)
    def _(c):
        for part in range(2):
            for j in range(WIDE):
                load_start(tile_of(part, c, j))

    barrier = pltpu.get_barrier_semaphore()
    peers = [at_x(1), at_x(3), at_y(1), at_y(3), partner, before, after]
    for peer in peers:
        pl.semaphore_signal(barrier, inc=1, device_id=peer, device_id_type=MESH)

    def make_acts(k):
        for kind in range(3):
            fetch(k, kind).wait()
        column = turned(x, order[k])

        @pl.loop(0, RING)
        def _(row):
            mine = layout_ref[0, row * RING + column] == my_expert
            held = [stage[k % 2, kind, row] for kind in range(3)]
            pair = swiglu_grads(*held, mine)
            acts[row, column, :, :, :hidden] = pair[0]
            acts[row, column, :, :, hidden:] = pair[1]

        if k + 2 < RING:
            for kind in range(3):
                fetch(k + 2, kind).start()

    def remote(src, dst, send, recv, device):
        return pltpu.make_async_remote_copy(
            src_ref=src, dst_ref=dst, send_sem=send, recv_sem=recv, device_id=device, device_id_type=MESH
        )

    def by_way(way):
        return 1 if way == 0 else 3

    def step1(part, c, way):
        return remote(
            first.at[part, c, way], second.at[part, c, way, way],
            send1.at[part, c, way], recv1.at[part, c, way], outer_device[part](by_way(way)),
        )

    def step2(part, c, way):
        return remote(
            second.at[part, c, way], third.at[part, c, way],
            send2.at[part, c, way], recv2.at[part, c, way], outer_device[part](by_way(way)),
        )

    def step3(part, c):
        return remote(
            third.at[part, c, 0, 1 - tensor], across.at[part, c], send3.at[part, c], recv3.at[part, c], partner
        )

    def step4(part, c, way):
        return remote(
            third.at[part, c, 0, tensor, turned(inner[part], 2), pl.ds(way * QUARTER, QUARTER)], near.at[part, c, way],
            send4.at[part, c, way], recv4.at[part, c, way], inner_device[part](by_way(way)),
        )

    def step5(part, c, way):
        return remote(
            third.at[part, c, 0, tensor, turned(inner[part], by_way(way))], far.at[part, c, way],
            send5.at[part, c, way], recv5.at[part, c, way], inner_device[part](by_way(way)),
        )

    def step6(part, c):
        return remote(
            far.at[part, c, 0], out_hbm.at[:, columns_of(tile_of(part, c, 0), WIDE)],
            send6.at[part, c], recv6.at[part, c], before,
        )

    def r_step0(part, c):
        return remote(halved.at[part, c], joined.at[part, c], r_send0.at[part, c], r_recv0.at[part, c], partner)

    def r_step1(part, c, way):
        return remote(
            r_first.at[part, c, pl.ds(2 * way, 2)], r_second.at[part, c, way, pl.ds(2 * way, 2)],
            r_send1.at[part, c, way], r_recv1.at[part, c, way], outer_device[part](by_way(way)),
        )

    def r_step2(part, c, way):
        return remote(
            r_second.at[part, c, way], r_third.at[part, c, way],
            r_send2.at[part, c, way], r_recv2.at[part, c, way], outer_device[part](by_way(way)),
        )

    def r_step4(part, c, way):
        return remote(
            r_third.at[part, c, 0, turned(inner[part], 2), pl.ds(way * QUARTER, QUARTER)], r_near.at[part, c, way],
            r_send4.at[part, c, way], r_recv4.at[part, c, way], inner_device[part](by_way(way)),
        )

    def r_step5(part, c, way):
        return remote(
            r_third.at[part, c, 0, turned(inner[part], by_way(way))], r_far.at[part, c, way],
            r_send5.at[part, c, way], r_recv5.at[part, c, way], inner_device[part](by_way(way)),
        )

    def r_step6(part, c):
        return remote(
            r_far.at[part, c, 0], out_hbm.at[:, columns_of(r_tile_of(part, c), 1)],
            r_send6.at[part, c], r_recv6.at[part, c], before,
        )

    def dot(rows, tile):
        rows = rows.reshape(-1, 2 * hidden)
        return jnp.dot(rows, weights[tile], preferred_element_type=jnp.float32)

    def product(part, c, chunk, j):
        rows = acts[:, chunk] if part == 0 else acts[chunk]
        return dot(rows, tile_of(part, c, j)).reshape(RING, 2, HALF, TILE), columns_of(j, 1)

    def r_product(part, c, chunk):
        rows = acts[:, chunk, tensor] if part == 0 else acts[chunk, :, tensor]
        held = joined[part, c, :, chunk] if part == 0 else joined[part, c, chunk]
        return dot(rows, r_tile_of(part, c)).reshape(RING, HALF, TILE) + held.astype(jnp.float32)

    def phase0(c):
        for part in range(2):
            for j in range(WIDE):
                load_wait(tile_of(part, c, j))

            @pl.loop(0, WIDE)
            def _(j):
                total, columns = product(part, c, turned(outer[part], 2), j)
                for way in range(2):
                    first[part, c, way, :, :, columns] = total[:, way].astype(jnp.bfloat16)

            for way in range(2):
                step1(part, c, way).start()

            if part == 0:

                @pl.when(c == 0)
                def _():
                    for k in range(1, RING):
                        make_acts(k)

    def phase1(c):
        for part in range(2):
            for way in range(2):
                step1(part, c, way).wait_recv()

                @pl.loop(0, WIDE)
                def _(j):
                    total, columns = product(part, c, turned(outer[part], by_way(way)), j)
                    held = second[part, c, way, way, :, :, columns].astype(jnp.float32)
                    second[part, c, way, way, :, :, columns] = (total[:, way] + held).astype(jnp.bfloat16)
                    second[part, c, way, 1 - way, :, :, columns] = total[:, 1 - way].astype(jnp.bfloat16)

                step2(part, c, way).start()

    def phase2(c):
        for part in range(2):
            for way in range(2):
                step2(part, c, way).wait_recv()

            @pl.loop(0, WIDE)
            def _(j):
                total, columns = product(part, c, outer[part], j)
                for half in range(2):
                    held = third[part, c, 0, half, :, :, columns].astype(jnp.float32)
                    held += third[part, c, 1, half, :, :, columns].astype(jnp.float32)
                    third[part, c, 0, half, :, :, columns] = (total[:, half] + held).astype(jnp.bfloat16)

            step3(part, c).start()

    def phase3(c):
        for part in range(2):
            step3(part, c).wait_recv()
            total = third[part, c, 0, tensor].astype(jnp.float32) + across[part, c].astype(jnp.float32)
            third[part, c, 0, tensor] = total.astype(jnp.bfloat16)
            for way in range(2):
                step4(part, c, way).start()

    def phase4(c):
        for part in range(2):
            for way in range(2):
                step4(part, c, way).wait_recv()
                spot = turned(inner[part], by_way(way))
                rows = pl.ds(way * QUARTER, QUARTER)
                total = third[part, c, 0, tensor, spot, rows].astype(jnp.float32)
                total += near[part, c, way].astype(jnp.float32)
                third[part, c, 0, tensor, spot, rows] = total.astype(jnp.bfloat16)
                step5(part, c, way).start()

    def phase5(c):
        for part in range(2):
            for way in range(2):
                step5(part, c, way).wait_recv()
            total = third[part, c, 0, tensor, inner[part]].astype(jnp.float32)
            total += far[part, c, 0].astype(jnp.float32)
            total += far[part, c, 1].astype(jnp.float32)
            far[part, c, 0] = total.astype(jnp.bfloat16)
            step6(part, c).start()

    def r_phase0(c):
        for part in range(2):
            load_wait(r_tile_of(part, c))
            total = dot(acts[:, :, 1 - tensor], r_tile_of(part, c))
            halved[part, c] = total.astype(jnp.bfloat16).reshape(RING, RING, HALF, TILE)
            r_step0(part, c).start()

    def r_phase1(c):
        for part in range(2):
            r_step0(part, c).wait_recv()
            r_first[part, c] = r_product(part, c, turned(outer[part], 2)).astype(jnp.bfloat16)
            for way in range(2):
                r_step1(part, c, way).start()

    def r_phase2(c):
        for part in range(2):
            for way in range(2):
                r_step1(part, c, way).wait_recv()
                total = r_product(part, c, turned(outer[part], by_way(way)))
                here, there = 2 * way, 2 * (1 - way)
                held = r_second[part, c, way, here : here + 2].astype(jnp.float32)
                r_second[part, c, way, here : here + 2] = (total[here : here + 2] + held).astype(jnp.bfloat16)
                r_second[part, c, way, there : there + 2] = total[there : there + 2].astype(jnp.bfloat16)
                r_step2(part, c, way).start()

    def r_phase3(c):
        for part in range(2):
            for way in range(2):
                r_step2(part, c, way).wait_recv()
            total = r_product(part, c, outer[part])
            total += r_third[part, c, 0].astype(jnp.float32)
            total += r_third[part, c, 1].astype(jnp.float32)
            r_third[part, c, 0] = total.astype(jnp.bfloat16)
            for way in range(2):
                r_step4(part, c, way).start()

    def r_phase4(c):
        for part in range(2):
            for way in range(2):
                r_step4(part, c, way).wait_recv()
                spot = turned(inner[part], by_way(way))
                rows = pl.ds(way * QUARTER, QUARTER)
                total = r_third[part, c, 0, spot, rows].astype(jnp.float32)
                total += r_near[part, c, way].astype(jnp.float32)
                r_third[part, c, 0, spot, rows] = total.astype(jnp.bfloat16)
                r_step5(part, c, way).start()

    def r_phase5(c):
        for part in range(2):
            for way in range(2):
                r_step5(part, c, way).wait_recv()
            total = r_third[part, c, 0, inner[part]].astype(jnp.float32)
            total += r_far[part, c, 0].astype(jnp.float32)
            total += r_far[part, c, 1].astype(jnp.float32)
            r_far[part, c, 0] = total.astype(jnp.bfloat16)
            r_step6(part, c).start()

    make_acts(0)
    pl.semaphore_wait(barrier, len(peers))

    phases = (phase0, phase1, phase2, phase3, phase4, phase5)
    r_phases = (r_phase0, r_phase1, r_phase2, r_phase3, r_phase4, r_phase5)

    @pl.loop(0, max(CHUNKS + LAGS[-1], R_CHUNKS + R_LAGS[-1]))
    def _(slot):
        for i in range(6):

            @pl.when((slot >= LAGS[i]) & (slot < CHUNKS + LAGS[i]))
            def _():
                phases[i](slot - LAGS[i])

            @pl.when((slot >= R_LAGS[i]) & (slot < R_CHUNKS + R_LAGS[i]))
            def _():
                r_phases[i](slot - R_LAGS[i])

    @pl.loop(0, CHUNKS)
    def _(c):
        for part in range(2):
            step6(part, c).wait()
            step3(part, c).wait_send()
            for way in range(2):
                for step in (step1, step2, step4, step5):
                    step(part, c, way).wait_send()

    @pl.loop(0, R_CHUNKS)
    def _(c):
        for part in range(2):
            r_step6(part, c).wait()
            r_step0(part, c).wait_send()
            for way in range(2):
                for step in (r_step1, r_step2, r_step4, r_step5):
                    step(part, c, way).wait_send()


def per_device(grad_hidden, gate_pre, up_pre, w_gate, w_up, block_expert):
    hidden, model = w_gate.shape[1:]
    rows = grad_hidden.shape[1]
    width = WIDE * TILE
    blocked = (RING, RING, 2, HALF, hidden)
    dma = pltpu.SemaphoreType.DMA
    anywhere = pl.BlockSpec(memory_space=pl.ANY)

    def room(*shape):
        return pltpu.VMEM(shape, jnp.bfloat16)

    both, single = dma((2, CHUNKS, 2)), dma((2, CHUNKS))
    r_both, r_single = dma((2, R_CHUNKS, 2)), dma((2, R_CHUNKS))
    out = pl.pallas_call(
        kernel,
        out_shape=jax.ShapeDtypeStruct((HALF, model), jnp.bfloat16),
        in_specs=[pl.BlockSpec(memory_space=pltpu.SMEM)] + [anywhere] * 5,
        out_specs=anywhere,
        scratch_shapes=[
            room(2, 3, RING, 2, HALF, hidden),
            room(RING, RING, 2, HALF, 2 * hidden),
            room(model // TILE, 2 * hidden, TILE),
            room(2, CHUNKS, 2, RING, HALF, width),
            room(2, CHUNKS, 2, 2, RING, HALF, width),
            room(2, CHUNKS, 2, 2, RING, HALF, width),
            room(2, CHUNKS, RING, HALF, width),
            room(2, CHUNKS, 2, QUARTER, width),
            room(2, CHUNKS, 2, HALF, width),
            room(2, R_CHUNKS, RING, RING, HALF, TILE),
            room(2, R_CHUNKS, RING, RING, HALF, TILE),
            room(2, R_CHUNKS, RING, HALF, TILE),
            room(2, R_CHUNKS, 2, RING, HALF, TILE),
            room(2, R_CHUNKS, 2, RING, HALF, TILE),
            room(2, R_CHUNKS, 2, QUARTER, TILE),
            room(2, R_CHUNKS, 2, HALF, TILE),
            dma((RING, 3)),
            dma((model // TILE, 2)),
        ]
        + [both] * 4
        + [single] * 2
        + [both] * 4
        + [single] * 2
        + [r_single] * 2
        + [r_both] * 8
        + [r_single] * 2,
        cost_estimate=pl.CostEstimate(
            flops=4 * rows * hidden * model, bytes_accessed=6 * hidden * rows + 4 * hidden * model, transcendentals=0
        ),
        compiler_params=pltpu.CompilerParams(
            collective_id=0, has_side_effects=True, vmem_limit_bytes=61 * 1024 * 1024
        ),
    )(
        block_expert,
        grad_hidden.reshape(blocked),
        gate_pre.reshape(blocked),
        up_pre.reshape(blocked),
        w_gate[0],
        w_up[0],
    )
    return out[None]


def solution(mesh):
    return jax.shard_map(
        per_device,
        mesh=mesh,
        in_specs=(
            P("section", None, ("dp", "tensor")),
            P("section", None, ("dp", "tensor")),
            P("section", None, ("dp", "tensor")),
            P("section", ("dp", "tensor"), None),
            P("section", ("dp", "tensor"), None),
            P("section", None),
        ),
        out_specs=P("section", ("dp", "tensor"), None),
        check_vma=False,
    )
```

```python
import jax
import jax.numpy as jnp
from jax import lax
from jax.experimental import pallas as pl
from jax.experimental.pallas import tpu as pltpu
from jax.sharding import PartitionSpec as P

F = 8192
BLOCK = 128
RING = 4
HALF = BLOCK // 2
QUARTER = HALF // 2
CHUNKS = 5
WIDE = 2
R_CHUNKS = 2
LAGS = (0, 2, 3, 5, 6, 7)
R_LAGS = (0, 4, 5, 6, 7, 9)
TILE = 256
STRIP = 16
UNROLL = 4
MESH = pl.DeviceIdType.MESH


def swiglu_grads(grad_rows, gate_rows, up_rows, mine):
    gate_f = gate_rows.astype(jnp.float32)
    half_tanh = 0.5 * jnp.tanh(0.5 * gate_f)
    grad_f = jnp.where(mine, grad_rows.astype(jnp.float32), 0.0)
    scaled = grad_f * (0.5 + half_tanh)
    grad_up = scaled * gate_f
    grad_gate = up_rows.astype(jnp.float32) * (scaled + grad_up * (0.5 - half_tanh))
    return grad_gate.astype(jnp.bfloat16), grad_up.astype(jnp.bfloat16)


def kernel(
    layout_ref, grad_hbm, gate_hbm, up_hbm, w_gate_hbm, w_up_hbm, out_hbm,
    stage, acts, weights,
    first, second, third, across, near, far,
    halved, joined, r_first, r_second, r_third, r_near, r_far,
    stage_sem, load_sem,
    send1, recv1, send2, recv2, send3, recv3, send4, recv4, send5, recv5, send6, recv6,
    r_send0, r_recv0, r_send1, r_recv1, r_send2, r_recv2, r_send4, r_recv4, r_send5, r_recv5, r_send6, r_recv6,
):
    section = lax.axis_index("section")
    dp = lax.axis_index("dp")
    tensor = lax.axis_index("tensor")
    y, x = dp // RING, dp % RING
    hidden = w_gate_hbm.shape[0]
    width = WIDE * TILE
    my_expert = (dp * 2 + tensor) * hidden // F

    def turned(value, by):
        return (value + by) % RING

    def at_x(by):
        return (section, y * RING + turned(x, by), tensor)

    def at_y(by):
        return (section, turned(y, by) * RING + x, tensor)

    outer = (x, y)
    inner = (y, x)
    outer_device = (at_x, at_y)
    inner_device = (at_y, at_x)
    partner = (section, dp, 1 - tensor)
    before = ((section + 3) % 4, dp, tensor)
    after = ((section + 1) % 4, dp, tensor)

    def fetch(k, kind):
        source = (grad_hbm, gate_hbm, up_hbm)[kind]
        return pltpu.make_async_copy(source.at[:, turned(x, k)], stage.at[k, kind], stage_sem.at[k, kind])

    def tile_of(part, c, j):
        return (part * CHUNKS + c) * WIDE + j

    def r_tile_of(part, c):
        return 2 * CHUNKS * WIDE + part * R_CHUNKS + c

    def columns_of(tile, count):
        return pl.ds(pl.multiple_of(tile * TILE, TILE), count * TILE)

    def load(tile, kind):
        source = (w_gate_hbm, w_up_hbm)[kind]
        return pltpu.make_async_copy(
            source.at[:, columns_of(tile, 1)],
            weights.at[tile, pl.ds(kind * hidden, hidden), :],
            load_sem.at[tile, kind],
        )

    def load_start(tile):
        for kind in range(2):
            load(tile, kind).start()

    def load_wait(tile):
        for kind in range(2):
            load(tile, kind).wait()

    barrier = pltpu.get_barrier_semaphore()
    peers = [at_x(1), at_x(3), at_y(1), at_y(3), partner, before, after]
    for peer in peers:
        pl.semaphore_signal(barrier, inc=1, device_id=peer, device_id_type=MESH)

    for kind in range(3):
        fetch(2, kind).start()
    for j in range(WIDE):
        load_start(tile_of(0, 0, j))
    for k in (0, 1, 3):
        for kind in range(3):
            fetch(k, kind).start()
    for j in range(WIDE):
        load_start(tile_of(1, 0, j))

    def load_rest():
        @pl.loop(0, R_CHUNKS)
        def _(c):
            for part in range(2):
                load_start(r_tile_of(part, c))

        @pl.loop(1, CHUNKS)
        def _(c):
            for part in range(2):
                for j in range(WIDE):
                    load_start(tile_of(part, c, j))

    def make_acts(down, along):
        row, column = turned(y, down), turned(x, along)
        mine = layout_ref[0, row * RING + column] == my_expert

        @pl.loop(0, 2 * HALF // STRIP // UNROLL)
        def _(i):
            for k in range(UNROLL):
                strip = i * UNROLL + k
                half = strip // (HALF // STRIP)
                rows = pl.ds(pl.multiple_of(strip % (HALF // STRIP) * STRIP, STRIP), STRIP)
                held = [stage[along, kind, row, half, rows] for kind in range(3)]
                pair = swiglu_grads(*held, mine)
                acts[row, column, half, rows, :hidden] = pair[0]
                acts[row, column, half, rows, hidden:] = pair[1]

    def remote(src, dst, send, recv, device):
        return pltpu.make_async_remote_copy(
            src_ref=src, dst_ref=dst, send_sem=send, recv_sem=recv, device_id=device, device_id_type=MESH
        )

    def by_way(way):
        return 1 if way == 0 else 3

    def step1(part, c, way):
        return remote(
            first.at[part, c, way], second.at[part, c, way, way],
            send1.at[part, c, way], recv1.at[part, c, way], outer_device[part](by_way(way)),
        )

    def step2(part, c, way):
        return remote(
            second.at[part, c, way], third.at[part, c, way],
            send2.at[part, c, way], recv2.at[part, c, way], outer_device[part](by_way(way)),
        )

    def step3(part, c):
        return remote(
            third.at[part, c, 0, 1 - tensor], across.at[part, c], send3.at[part, c], recv3.at[part, c], partner
        )

    def step4(part, c, way):
        return remote(
            third.at[part, c, 0, tensor, turned(inner[part], 2), pl.ds(way * QUARTER, QUARTER)], near.at[part, c, way],
            send4.at[part, c, way], recv4.at[part, c, way], inner_device[part](by_way(way)),
        )

    def step5(part, c, way):
        return remote(
            third.at[part, c, 0, tensor, turned(inner[part], by_way(way))], far.at[part, c, way],
            send5.at[part, c, way], recv5.at[part, c, way], inner_device[part](by_way(way)),
        )

    def step6(part, c):
        return remote(
            far.at[part, c, 0], out_hbm.at[:, columns_of(tile_of(part, c, 0), WIDE)],
            send6.at[part, c], recv6.at[part, c], before,
        )

    def r_step0(part, c):
        return remote(halved.at[part, c], joined.at[part, c], r_send0.at[part, c], r_recv0.at[part, c], partner)

    def r_step1(part, c, way):
        return remote(
            r_first.at[part, c, pl.ds(2 * way, 2)], r_second.at[part, c, way, pl.ds(2 * way, 2)],
            r_send1.at[part, c, way], r_recv1.at[part, c, way], outer_device[part](by_way(way)),
        )

    def r_step2(part, c, way):
        return remote(
            r_second.at[part, c, way], r_third.at[part, c, way],
            r_send2.at[part, c, way], r_recv2.at[part, c, way], outer_device[part](by_way(way)),
        )

    def r_step4(part, c, way):
        return remote(
            r_third.at[part, c, 0, turned(inner[part], 2), pl.ds(way * QUARTER, QUARTER)], r_near.at[part, c, way],
            r_send4.at[part, c, way], r_recv4.at[part, c, way], inner_device[part](by_way(way)),
        )

    def r_step5(part, c, way):
        return remote(
            r_third.at[part, c, 0, turned(inner[part], by_way(way))], r_far.at[part, c, way],
            r_send5.at[part, c, way], r_recv5.at[part, c, way], inner_device[part](by_way(way)),
        )

    def r_step6(part, c):
        return remote(
            r_far.at[part, c, 0], out_hbm.at[:, columns_of(r_tile_of(part, c), 1)],
            r_send6.at[part, c], r_recv6.at[part, c], before,
        )

    def dot(rows, tile):
        rows = rows.reshape(-1, 2 * hidden)
        return jnp.dot(rows, weights[tile], preferred_element_type=jnp.float32)

    def product(part, c, chunk, j):
        rows = acts[:, chunk] if part == 0 else acts[chunk]
        return dot(rows, tile_of(part, c, j)).reshape(RING, 2, HALF, TILE), columns_of(j, 1)

    def r_product(part, c, chunk):
        rows = acts[:, chunk, tensor] if part == 0 else acts[chunk, :, tensor]
        held = joined[part, c, :, chunk] if part == 0 else joined[part, c, chunk]
        return dot(rows, r_tile_of(part, c)).reshape(RING, HALF, TILE) + held.astype(jnp.float32)

    def phase0(c):
        for part in range(2):
            for j in range(WIDE):
                load_wait(tile_of(part, c, j))

            @pl.loop(0, WIDE)
            def _(j):
                total, columns = product(part, c, turned(outer[part], 2), j)
                for way in range(2):
                    first[part, c, way, :, :, columns] = total[:, way].astype(jnp.bfloat16)

            for way in range(2):
                step1(part, c, way).start()

            if part == 0:

                @pl.when(c == 0)
                def _():
                    load_rest()
                    for k in (0, 1, 3):
                        for kind in range(3):
                            fetch(k, kind).wait()

                    @pl.loop(0, 3)
                    def _(i):
                        make_acts(2, turned(i, 3))

    def phase1(c):
        for part in range(2):
            for way in range(2):
                step1(part, c, way).wait_recv()

                @pl.loop(0, WIDE)
                def _(j):
                    total, columns = product(part, c, turned(outer[part], by_way(way)), j)
                    held = second[part, c, way, way, :, :, columns].astype(jnp.float32)
                    second[part, c, way, way, :, :, columns] = (total[:, way] + held).astype(jnp.bfloat16)
                    second[part, c, way, 1 - way, :, :, columns] = total[:, 1 - way].astype(jnp.bfloat16)

                step2(part, c, way).start()

    def phase2(c):
        for part in range(2):
            for way in range(2):
                step2(part, c, way).wait_recv()

            @pl.loop(0, WIDE)
            def _(j):
                total, columns = product(part, c, outer[part], j)
                for half in range(2):
                    held = third[part, c, 0, half, :, :, columns].astype(jnp.float32)
                    held += third[part, c, 1, half, :, :, columns].astype(jnp.float32)
                    third[part, c, 0, half, :, :, columns] = (total[:, half] + held).astype(jnp.bfloat16)

            step3(part, c).start()

    def phase3(c):
        for part in range(2):
            step3(part, c).wait_recv()
            total = third[part, c, 0, tensor].astype(jnp.float32) + across[part, c].astype(jnp.float32)
            third[part, c, 0, tensor] = total.astype(jnp.bfloat16)
            for way in range(2):
                step4(part, c, way).start()

    def phase4(c):
        for part in range(2):
            for way in range(2):
                step4(part, c, way).wait_recv()
                spot = turned(inner[part], by_way(way))
                rows = pl.ds(way * QUARTER, QUARTER)
                total = third[part, c, 0, tensor, spot, rows].astype(jnp.float32)
                total += near[part, c, way].astype(jnp.float32)
                third[part, c, 0, tensor, spot, rows] = total.astype(jnp.bfloat16)
                step5(part, c, way).start()

    def phase5(c):
        for part in range(2):
            for way in range(2):
                step5(part, c, way).wait_recv()
            total = third[part, c, 0, tensor, inner[part]].astype(jnp.float32)
            total += far[part, c, 0].astype(jnp.float32)
            total += far[part, c, 1].astype(jnp.float32)
            far[part, c, 0] = total.astype(jnp.bfloat16)
            step6(part, c).start()

    def r_phase0(c):
        @pl.when(c == 0)
        def _():
            @pl.loop(0, 9)
            def _(i):
                make_acts(turned(i // 3, 3), turned(i % 3, 3))

        for part in range(2):
            load_wait(r_tile_of(part, c))
            total = dot(acts[:, :, 1 - tensor], r_tile_of(part, c))
            halved[part, c] = total.astype(jnp.bfloat16).reshape(RING, RING, HALF, TILE)
            r_step0(part, c).start()

    def r_phase1(c):
        for part in range(2):
            r_step0(part, c).wait_recv()
            r_first[part, c] = r_product(part, c, turned(outer[part], 2)).astype(jnp.bfloat16)
            for way in range(2):
                r_step1(part, c, way).start()

    def r_phase2(c):
        for part in range(2):
            for way in range(2):
                r_step1(part, c, way).wait_recv()
                total = r_product(part, c, turned(outer[part], by_way(way)))
                here, there = 2 * way, 2 * (1 - way)
                held = r_second[part, c, way, here : here + 2].astype(jnp.float32)
                r_second[part, c, way, here : here + 2] = (total[here : here + 2] + held).astype(jnp.bfloat16)
                r_second[part, c, way, there : there + 2] = total[there : there + 2].astype(jnp.bfloat16)
                r_step2(part, c, way).start()

    def r_phase3(c):
        for part in range(2):
            for way in range(2):
                r_step2(part, c, way).wait_recv()
            total = r_product(part, c, outer[part])
            total += r_third[part, c, 0].astype(jnp.float32)
            total += r_third[part, c, 1].astype(jnp.float32)
            r_third[part, c, 0] = total.astype(jnp.bfloat16)
            for way in range(2):
                r_step4(part, c, way).start()

    def r_phase4(c):
        for part in range(2):
            for way in range(2):
                r_step4(part, c, way).wait_recv()
                spot = turned(inner[part], by_way(way))
                rows = pl.ds(way * QUARTER, QUARTER)
                total = r_third[part, c, 0, spot, rows].astype(jnp.float32)
                total += r_near[part, c, way].astype(jnp.float32)
                r_third[part, c, 0, spot, rows] = total.astype(jnp.bfloat16)
                r_step5(part, c, way).start()

    def r_phase5(c):
        for part in range(2):
            for way in range(2):
                r_step5(part, c, way).wait_recv()
            total = r_third[part, c, 0, inner[part]].astype(jnp.float32)
            total += r_far[part, c, 0].astype(jnp.float32)
            total += r_far[part, c, 1].astype(jnp.float32)
            r_far[part, c, 0] = total.astype(jnp.bfloat16)
            r_step6(part, c).start()

    for kind in range(3):
        fetch(2, kind).wait()

    @pl.loop(0, RING)
    def _(i):
        make_acts(i, 2)

    pl.semaphore_wait(barrier, len(peers))

    phases = (phase0, phase1, phase2, phase3, phase4, phase5)
    r_phases = (r_phase0, r_phase1, r_phase2, r_phase3, r_phase4, r_phase5)

    @pl.loop(0, max(CHUNKS + LAGS[-1], R_CHUNKS + R_LAGS[-1]))
    def _(slot):
        for i in range(6):

            @pl.when((slot >= LAGS[i]) & (slot < CHUNKS + LAGS[i]))
            def _():
                phases[i](slot - LAGS[i])

            @pl.when((slot >= R_LAGS[i]) & (slot < R_CHUNKS + R_LAGS[i]))
            def _():
                r_phases[i](slot - R_LAGS[i])

    @pl.loop(0, CHUNKS)
    def _(c):
        for part in range(2):
            step6(part, c).wait()
            step3(part, c).wait_send()
            for way in range(2):
                for step in (step1, step2, step4, step5):
                    step(part, c, way).wait_send()

    @pl.loop(0, R_CHUNKS)
    def _(c):
        for part in range(2):
            r_step6(part, c).wait()
            r_step0(part, c).wait_send()
            for way in range(2):
                for step in (r_step1, r_step2, r_step4, r_step5):
                    step(part, c, way).wait_send()


def per_device(grad_hidden, gate_pre, up_pre, w_gate, w_up, block_expert):
    hidden, model = w_gate.shape[1:]
    rows = grad_hidden.shape[1]
    width = WIDE * TILE
    blocked = (RING, RING, 2, HALF, hidden)
    dma = pltpu.SemaphoreType.DMA
    anywhere = pl.BlockSpec(memory_space=pl.ANY)

    def room(*shape):
        return pltpu.VMEM(shape, jnp.bfloat16)

    both, single = dma((2, CHUNKS, 2)), dma((2, CHUNKS))
    r_both, r_single = dma((2, R_CHUNKS, 2)), dma((2, R_CHUNKS))
    out = pl.pallas_call(
        kernel,
        out_shape=jax.ShapeDtypeStruct((HALF, model), jnp.bfloat16),
        in_specs=[pl.BlockSpec(memory_space=pltpu.SMEM)] + [anywhere] * 5,
        out_specs=anywhere,
        scratch_shapes=[
            room(RING, 3, RING, 2, HALF, hidden),
            room(RING, RING, 2, HALF, 2 * hidden),
            room(model // TILE, 2 * hidden, TILE),
            room(2, CHUNKS, 2, RING, HALF, width),
            room(2, CHUNKS, 2, 2, RING, HALF, width),
            room(2, CHUNKS, 2, 2, RING, HALF, width),
            room(2, CHUNKS, RING, HALF, width),
            room(2, CHUNKS, 2, QUARTER, width),
            room(2, CHUNKS, 2, HALF, width),
            room(2, R_CHUNKS, RING, RING, HALF, TILE),
            room(2, R_CHUNKS, RING, RING, HALF, TILE),
            room(2, R_CHUNKS, RING, HALF, TILE),
            room(2, R_CHUNKS, 2, RING, HALF, TILE),
            room(2, R_CHUNKS, 2, RING, HALF, TILE),
            room(2, R_CHUNKS, 2, QUARTER, TILE),
            room(2, R_CHUNKS, 2, HALF, TILE),
            dma((RING, 3)),
            dma((model // TILE, 2)),
        ]
        + [both] * 4
        + [single] * 2
        + [both] * 4
        + [single] * 2
        + [r_single] * 2
        + [r_both] * 8
        + [r_single] * 2,
        cost_estimate=pl.CostEstimate(
            flops=4 * rows * hidden * model, bytes_accessed=6 * hidden * rows + 4 * hidden * model, transcendentals=0
        ),
        compiler_params=pltpu.CompilerParams(
            collective_id=0, has_side_effects=True, vmem_limit_bytes=61 * 1024 * 1024
        ),
    )(
        block_expert,
        grad_hidden.reshape(blocked),
        gate_pre.reshape(blocked),
        up_pre.reshape(blocked),
        w_gate[0],
        w_up[0],
    )
    return out[None]


def solution(mesh):
    return jax.shard_map(
        per_device,
        mesh=mesh,
        in_specs=(
            P("section", None, ("dp", "tensor")),
            P("section", None, ("dp", "tensor")),
            P("section", None, ("dp", "tensor")),
            P("section", ("dp", "tensor"), None),
            P("section", ("dp", "tensor"), None),
            P("section", None),
        ),
        out_specs=P("section", ("dp", "tensor"), None),
        check_vma=False,
    )
```

```python
import jax
import jax.numpy as jnp
from jax import lax
from jax.experimental import pallas as pl
from jax.experimental.pallas import tpu as pltpu
from jax.sharding import PartitionSpec as P

F = 8192
BLOCK = 128
RING = 4
HALF = BLOCK // 2
QUARTER = HALF // 2
CHUNKS = 5
LAST = CHUNKS - 1
LAGS = (0, 2, 4, 6, 8, 10)
R_LAGS = (0, 6, 8, 10, 12, 17)
A_LAGS = (8, 10, 12)
TILE = 512
STRIP = 16
UNROLL = 4
MESH = pl.DeviceIdType.MESH


def swiglu_grads(grad_rows, gate_rows, up_rows, mine):
    gate_f = gate_rows.astype(jnp.float32)
    half_tanh = 0.5 * jnp.tanh(0.5 * gate_f)
    grad_f = jnp.where(mine, grad_rows.astype(jnp.float32), 0.0)
    scaled = grad_f * (0.5 + half_tanh)
    grad_up = scaled * gate_f
    grad_gate = up_rows.astype(jnp.float32) * (scaled + grad_up * (0.5 - half_tanh))
    return grad_gate.astype(jnp.bfloat16), grad_up.astype(jnp.bfloat16)


def kernel(
    layout_ref, grad_hbm, gate_hbm, up_hbm, w_gate_hbm, w_up_hbm, out_hbm,
    stage, acts, weights,
    first, second, third, across, near, far,
    halved, joined, r_first, r_second, r_third, r_near, r_far, a_near, a_far, a_last,
    stage_sem, load_sem,
    send1, recv1, send2, recv2, send3, recv3, send4, recv4, send5, recv5, send6, recv6,
    r_send0, r_recv0, r_send1, r_recv1, r_send2, r_recv2, r_send4, r_recv4, r_send5, r_recv5, r_send6, r_recv6,
    a_send4, a_recv4, a_send5, a_recv5, a_send6, a_recv6, out_sem,
):
    section = lax.axis_index("section")
    dp = lax.axis_index("dp")
    tensor = lax.axis_index("tensor")
    y, x = dp // RING, dp % RING
    hidden = w_gate_hbm.shape[0]
    my_expert = (dp * 2 + tensor) * hidden // F

    def turned(value, by):
        return (value + by) % RING

    xs = [turned(x, by) for by in range(RING)]
    ys = [turned(y, by) for by in range(RING)]
    x_devices = [(section, y * RING + xs[by], tensor) for by in range(RING)]
    y_devices = [(section, ys[by] * RING + x, tensor) for by in range(RING)]

    outer = (xs, ys)
    inner = (ys, xs)
    outer_device = (x_devices, y_devices)
    inner_device = (y_devices, x_devices)
    partner = (section, dp, 1 - tensor)
    before = ((section + 3) % 4, dp, tensor)

    def fetch(k, kind):
        source = (grad_hbm, gate_hbm, up_hbm)[kind]
        return pltpu.make_async_copy(source.at[:, xs[k]], stage.at[k, kind], stage_sem.at[k, kind])

    def tile_of(part, c):
        return part * CHUNKS + c

    def r_tile_of(part):
        return 2 * CHUNKS + part

    def columns_of(tile):
        return pl.ds(pl.multiple_of(tile * TILE, TILE), TILE)

    def load(tile, kind):
        source = (w_gate_hbm, w_up_hbm)[kind]
        return pltpu.make_async_copy(
            source.at[:, columns_of(tile)],
            weights.at[tile, pl.ds(kind * hidden, hidden), :],
            load_sem.at[tile, kind],
        )

    def load_start(tile):
        for kind in range(2):
            load(tile, kind).start()

    def load_wait(tile):
        for kind in range(2):
            load(tile, kind).wait()

    barrier = pltpu.get_barrier_semaphore()
    peers = [x_devices[1], x_devices[3], y_devices[1], y_devices[3], partner]
    peers += [((section + by) % 4, dp, half) for by in (1, 3) for half in range(2)]
    for peer in peers:
        pl.semaphore_signal(barrier, inc=1, device_id=peer, device_id_type=MESH)

    for kind in range(3):
        fetch(2, kind).start()
    load_start(tile_of(0, 0))
    for k in (0, 1, 3):
        for kind in range(3):
            fetch(k, kind).start()
    load_start(tile_of(1, 0))

    def load_rest():
        for part in range(2):
            load_start(r_tile_of(part))

        @pl.loop(1, CHUNKS)
        def _(c):
            for part in range(2):
                load_start(tile_of(part, c))

    def make_acts(down, along):
        row, column = turned(y, down), turned(x, along)
        mine = layout_ref[0, row * RING + column] == my_expert

        @pl.loop(0, 2 * HALF // STRIP // UNROLL)
        def _(i):
            for k in range(UNROLL):
                strip = i * UNROLL + k
                half = strip // (HALF // STRIP)
                rows = pl.ds(pl.multiple_of(strip % (HALF // STRIP) * STRIP, STRIP), STRIP)
                held = [stage[along, kind, row, half, rows] for kind in range(3)]
                pair = swiglu_grads(*held, mine)
                acts[row, column, half, rows, :hidden] = pair[0]
                acts[row, column, half, rows, hidden:] = pair[1]

    def remote(src, dst, send, recv, device):
        return pltpu.make_async_remote_copy(
            src_ref=src, dst_ref=dst, send_sem=send, recv_sem=recv, device_id=device, device_id_type=MESH
        )

    def by_way(way):
        return 1 if way == 0 else 3

    def step1(part, c, way):
        return remote(
            first.at[part, c, way], second.at[part, c, way, way],
            send1.at[part, c, way], recv1.at[part, c, way], outer_device[part][by_way(way)],
        )

    def step2(part, c, way):
        return remote(
            second.at[part, c, way], third.at[part, c, way],
            send2.at[part, c, way], recv2.at[part, c, way], outer_device[part][by_way(way)],
        )

    def step3(part, c):
        return remote(
            third.at[part, c, 0, 1 - tensor], across.at[part, c], send3.at[part, c], recv3.at[part, c], partner
        )

    def step4(part, c, way):
        return remote(
            third.at[part, c, 0, tensor, inner[part][2], pl.ds(way * QUARTER, QUARTER)], near.at[part, c, way],
            send4.at[part, c, way], recv4.at[part, c, way], inner_device[part][by_way(way)],
        )

    def step5(part, c, way):
        return remote(
            third.at[part, c, 0, tensor, inner[part][by_way(way)]], far.at[part, c, way],
            send5.at[part, c, way], recv5.at[part, c, way], inner_device[part][by_way(way)],
        )

    def step6(part, c):
        return remote(
            far.at[part, c, 0], out_hbm.at[:, columns_of(tile_of(part, c))],
            send6.at[part, c], recv6.at[part, c], before,
        )

    def r_step0(part):
        return remote(halved.at[part], joined.at[part], r_send0.at[part], r_recv0.at[part], partner)

    def r_step1(part, way):
        return remote(
            r_first.at[part, pl.ds(2 * way, 2)], r_second.at[part, way, pl.ds(2 * way, 2)],
            r_send1.at[part, way], r_recv1.at[part, way], outer_device[part][by_way(way)],
        )

    def r_step2(part, way):
        return remote(
            r_second.at[part, way], r_third.at[part, way],
            r_send2.at[part, way], r_recv2.at[part, way], outer_device[part][by_way(way)],
        )

    def r_step4(part, way):
        return remote(
            r_third.at[part, 0, inner[part][2], pl.ds(way * QUARTER, QUARTER)], r_near.at[part, way],
            r_send4.at[part, way], r_recv4.at[part, way], inner_device[part][by_way(way)],
        )

    def r_step5(part, way):
        return remote(
            r_third.at[part, 0, inner[part][by_way(way)]], r_far.at[part, way],
            r_send5.at[part, way], r_recv5.at[part, way], inner_device[part][by_way(way)],
        )

    def r_step6(part):
        return remote(
            r_far.at[part, 0], out_hbm.at[:, columns_of(r_tile_of(part))],
            r_send6.at[part], r_recv6.at[part], before,
        )

    def a_step4(part, way):
        return remote(
            third.at[part, LAST, 0, way, inner[part][2]], a_near.at[part, way],
            a_send4.at[part, way], a_recv4.at[part, way], inner_device[part][by_way(way)],
        )

    def a_step5(part, way):
        return remote(
            third.at[part, LAST, 0, :, inner[part][by_way(way)]], a_far.at[part, way],
            a_send5.at[part, way], a_recv5.at[part, way], inner_device[part][by_way(way)],
        )

    def a_step6(part, half, source):
        return remote(
            third.at[part, LAST, 0, half, inner[part][0]], a_last.at[part, source],
            a_send6.at[part, half], a_recv6.at[part, source], ((section + 3) % 4, dp, half),
        )

    def a_out(part):
        return pltpu.make_async_copy(
            a_last.at[part, 0], out_hbm.at[:, columns_of(tile_of(part, LAST))], out_sem.at[part]
        )

    def dot(rows, tile):
        rows = rows.reshape(-1, 2 * hidden)
        return jnp.dot(rows, weights[tile], preferred_element_type=jnp.float32)

    def product(part, c, chunk):
        rows = acts[:, chunk] if part == 0 else acts[chunk]
        return dot(rows, tile_of(part, c)).reshape(RING, 2, HALF, TILE)

    def r_product(part, chunk):
        rows = acts[:, chunk, tensor] if part == 0 else acts[chunk, :, tensor]
        held = joined[part, :, chunk] if part == 0 else joined[part, chunk]
        return dot(rows, r_tile_of(part)).reshape(RING, HALF, TILE) + held.astype(jnp.float32)

    def phase0(c):
        for part in range(2):
            load_wait(tile_of(part, c))
            total = product(part, c, outer[part][2]).astype(jnp.bfloat16)
            for way in range(2):
                first[part, c, way] = total[:, way]
                step1(part, c, way).start()

            if part == 0:

                @pl.when(c == 0)
                def _():
                    load_rest()
                    for k in (0, 1, 3):
                        for kind in range(3):
                            fetch(k, kind).wait()

                    @pl.loop(0, 3)
                    def _(i):
                        make_acts(2, turned(i, 3))

    def phase1(c):
        for part in range(2):
            for way in range(2):
                step1(part, c, way).wait_recv()
                total = product(part, c, outer[part][by_way(way)])
                held = second[part, c, way, way].astype(jnp.float32)
                second[part, c, way, way] = (total[:, way] + held).astype(jnp.bfloat16)
                second[part, c, way, 1 - way] = total[:, 1 - way].astype(jnp.bfloat16)
                step2(part, c, way).start()

    def phase2(c):
        for part in range(2):
            for way in range(2):
                step2(part, c, way).wait_recv()
            total = product(part, c, outer[part][0])
            for half in range(2):
                held = third[part, c, 0, half].astype(jnp.float32) + third[part, c, 1, half].astype(jnp.float32)
                third[part, c, 0, half] = (total[:, half] + held).astype(jnp.bfloat16)

            @pl.when(c < LAST)
            def _():
                step3(part, c).start()

            @pl.when(c == LAST)
            def _():
                for way in range(2):
                    a_step4(part, way).start()

    def phase3(c):
        for part in range(2):
            step3(part, c).wait_recv()
            total = third[part, c, 0, tensor].astype(jnp.float32) + across[part, c].astype(jnp.float32)
            third[part, c, 0, tensor] = total.astype(jnp.bfloat16)
            for way in range(2):
                step4(part, c, way).start()

    def phase4(c):
        for part in range(2):
            for way in range(2):
                step4(part, c, way).wait_recv()
                spot = inner[part][by_way(way)]
                rows = pl.ds(way * QUARTER, QUARTER)
                total = third[part, c, 0, tensor, spot, rows].astype(jnp.float32)
                total += near[part, c, way].astype(jnp.float32)
                third[part, c, 0, tensor, spot, rows] = total.astype(jnp.bfloat16)
                step5(part, c, way).start()

    def phase5(c):
        for part in range(2):
            for way in range(2):
                step5(part, c, way).wait_recv()
            total = third[part, c, 0, tensor, inner[part][0]].astype(jnp.float32)
            total += far[part, c, 0].astype(jnp.float32)
            total += far[part, c, 1].astype(jnp.float32)
            far[part, c, 0] = total.astype(jnp.bfloat16)
            step6(part, c).start()

    def r_phase0():
        @pl.loop(0, 9)
        def _(i):
            make_acts(turned(i // 3, 3), turned(i % 3, 3))

        for part in range(2):
            load_wait(r_tile_of(part))
            for k in range(2):
                total = dot(acts[2 * k : 2 * k + 2, :, 1 - tensor], r_tile_of(part)).astype(jnp.bfloat16)
                halved[part, 2 * k : 2 * k + 2] = total.reshape(2, RING, HALF, TILE)
            r_step0(part).start()

    def r_phase1():
        for part in range(2):
            r_step0(part).wait_recv()
            r_first[part] = r_product(part, outer[part][2]).astype(jnp.bfloat16)
            for way in range(2):
                r_step1(part, way).start()

    def r_phase2():
        for part in range(2):
            for way in range(2):
                r_step1(part, way).wait_recv()
                total = r_product(part, outer[part][by_way(way)])
                here, there = 2 * way, 2 * (1 - way)
                held = r_second[part, way, here : here + 2].astype(jnp.float32)
                r_second[part, way, here : here + 2] = (total[here : here + 2] + held).astype(jnp.bfloat16)
                r_second[part, way, there : there + 2] = total[there : there + 2].astype(jnp.bfloat16)
                r_step2(part, way).start()

    def r_phase3():
        for part in range(2):
            for way in range(2):
                r_step2(part, way).wait_recv()
            total = r_product(part, outer[part][0])
            total += r_third[part, 0].astype(jnp.float32)
            total += r_third[part, 1].astype(jnp.float32)
            r_third[part, 0] = total.astype(jnp.bfloat16)
            for way in range(2):
                r_step4(part, way).start()

    def r_phase4():
        for part in range(2):
            for way in range(2):
                r_step4(part, way).wait_recv()
                spot = inner[part][by_way(way)]
                rows = pl.ds(way * QUARTER, QUARTER)
                total = r_third[part, 0, spot, rows].astype(jnp.float32)
                total += r_near[part, way].astype(jnp.float32)
                r_third[part, 0, spot, rows] = total.astype(jnp.bfloat16)
                r_step5(part, way).start()

    def r_phase5():
        for part in range(2):
            for way in range(2):
                r_step5(part, way).wait_recv()
            total = r_third[part, 0, inner[part][0]].astype(jnp.float32)
            total += r_far[part, 0].astype(jnp.float32)
            total += r_far[part, 1].astype(jnp.float32)
            r_far[part, 0] = total.astype(jnp.bfloat16)
            r_step6(part).start()

    def a_phase3():
        for part in range(2):
            for way in range(2):
                a_step4(part, way).wait_recv()
                spot = inner[part][by_way(way)]
                total = third[part, LAST, 0, way, spot].astype(jnp.float32) + a_near[part, way].astype(jnp.float32)
                third[part, LAST, 0, way, spot] = total.astype(jnp.bfloat16)
                a_step5(part, way).start()

    def a_phase4():
        for part in range(2):
            for way in range(2):
                a_step5(part, way).wait_recv()
            for half in range(2):
                total = third[part, LAST, 0, half, inner[part][0]].astype(jnp.float32)
                total += a_far[part, 0, half].astype(jnp.float32)
                total += a_far[part, 1, half].astype(jnp.float32)
                third[part, LAST, 0, half, inner[part][0]] = total.astype(jnp.bfloat16)
                a_step6(part, half, tensor).start()

    def a_phase5():
        for part in range(2):
            for source in range(2):
                a_step6(part, 0, source).wait_recv()
            total = a_last[part, 0].astype(jnp.float32) + a_last[part, 1].astype(jnp.float32)
            a_last[part, 0] = total.astype(jnp.bfloat16)
            a_out(part).start()

    for kind in range(3):
        fetch(2, kind).wait()

    @pl.loop(0, RING)
    def _(i):
        make_acts(i, 2)

    pl.semaphore_wait(barrier, len(peers))

    phases = (phase0, phase1, phase2, phase3, phase4, phase5)
    r_phases = (r_phase0, r_phase1, r_phase2, r_phase3, r_phase4, r_phase5)
    a_phases = (a_phase3, a_phase4, a_phase5)

    @pl.loop(0, max(LAST + LAGS[-1], R_LAGS[-1] + 1, A_LAGS[-1] + 1))
    def _(slot):
        for i in range(6):
            count = CHUNKS if i < 3 else LAST

            @pl.when((slot >= LAGS[i]) & (slot < count + LAGS[i]))
            def _():
                phases[i](slot - LAGS[i])

            if i >= 3:
                pl.when(slot == A_LAGS[i - 3])(a_phases[i - 3])

            pl.when(slot == R_LAGS[i])(r_phases[i])

    @pl.loop(0, CHUNKS)
    def _(c):
        for part in range(2):
            for way in range(2):
                for step in (step1, step2):
                    step(part, c, way).wait_send()

    @pl.loop(0, LAST)
    def _(c):
        for part in range(2):
            step6(part, c).wait()
            step3(part, c).wait_send()
            for way in range(2):
                for step in (step4, step5):
                    step(part, c, way).wait_send()

    for part in range(2):
        a_out(part).wait()
        r_step6(part).wait()
        r_step0(part).wait_send()
        for way in range(2):
            for step in (r_step1, r_step2, r_step4, r_step5, a_step4, a_step5):
                step(part, way).wait_send()
            a_step6(part, way, tensor).wait_send()


def per_device(grad_hidden, gate_pre, up_pre, w_gate, w_up, block_expert):
    hidden, model = w_gate.shape[1:]
    rows = grad_hidden.shape[1]
    blocked = (RING, RING, 2, HALF, hidden)
    dma = pltpu.SemaphoreType.DMA
    anywhere = pl.BlockSpec(memory_space=pl.ANY)

    def room(*shape):
        return pltpu.VMEM(shape, jnp.bfloat16)

    both, single = dma((2, CHUNKS, 2)), dma((2, CHUNKS))
    pairs, two = dma((2, 2)), dma((2,))
    out = pl.pallas_call(
        kernel,
        out_shape=jax.ShapeDtypeStruct((HALF, model), jnp.bfloat16),
        in_specs=[pl.BlockSpec(memory_space=pltpu.SMEM)] + [anywhere] * 5,
        out_specs=anywhere,
        scratch_shapes=[
            room(RING, 3, RING, 2, HALF, hidden),
            room(RING, RING, 2, HALF, 2 * hidden),
            room(model // TILE, 2 * hidden, TILE),
            room(2, CHUNKS, 2, RING, HALF, TILE),
            room(2, CHUNKS, 2, 2, RING, HALF, TILE),
            room(2, CHUNKS, 2, 2, RING, HALF, TILE),
            room(2, LAST, RING, HALF, TILE),
            room(2, LAST, 2, QUARTER, TILE),
            room(2, LAST, 2, HALF, TILE),
            room(2, RING, RING, HALF, TILE),
            room(2, RING, RING, HALF, TILE),
            room(2, RING, HALF, TILE),
            room(2, 2, RING, HALF, TILE),
            room(2, 2, RING, HALF, TILE),
            room(2, 2, QUARTER, TILE),
            room(2, 2, HALF, TILE),
            room(2, 2, HALF, TILE),
            room(2, 2, 2, HALF, TILE),
            room(2, 2, HALF, TILE),
            dma((RING, 3)),
            dma((model // TILE, 2)),
        ]
        + [both] * 4
        + [single] * 2
        + [both] * 4
        + [single] * 2
        + [two] * 2
        + [pairs] * 8
        + [two] * 2
        + [pairs] * 6
        + [two],
        cost_estimate=pl.CostEstimate(
            flops=4 * rows * hidden * model, bytes_accessed=6 * hidden * rows + 4 * hidden * model, transcendentals=0
        ),
        compiler_params=pltpu.CompilerParams(
            collective_id=0, has_side_effects=True, vmem_limit_bytes=61 * 1024 * 1024
        ),
    )(
        block_expert,
        grad_hidden.reshape(blocked),
        gate_pre.reshape(blocked),
        up_pre.reshape(blocked),
        w_gate[0],
        w_up[0],
    )
    return out[None]


def solution(mesh):
    return jax.shard_map(
        per_device,
        mesh=mesh,
        in_specs=(
            P("section", None, ("dp", "tensor")),
            P("section", None, ("dp", "tensor")),
            P("section", None, ("dp", "tensor")),
            P("section", ("dp", "tensor"), None),
            P("section", ("dp", "tensor"), None),
            P("section", None),
        ),
        out_specs=P("section", ("dp", "tensor"), None),
        check_vma=False,
    )
```

```python
import jax
import jax.numpy as jnp
from jax import lax
from jax.experimental import pallas as pl
from jax.experimental.pallas import tpu as pltpu
from jax.sharding import PartitionSpec as P

F = 8192
BLOCK = 128
RING = 4
HALF = BLOCK // 2
QUARTER = HALF // 2
CHUNKS = 5
LAST = CHUNKS - 1
LAGS = (0, 1, 3, 5, 7, 9)
R_LAGS = (0, 5, 7, 9, 11, 14)
A_LAGS = (7, 9, 14)
TILE = 512
STRIP = 16
UNROLL = 4
MESH = pl.DeviceIdType.MESH


def swiglu_grads(grad_rows, gate_rows, up_rows, mine):
    gate_f = gate_rows.astype(jnp.float32)
    half_tanh = 0.5 * jnp.tanh(0.5 * gate_f)
    grad_f = jnp.where(mine, grad_rows.astype(jnp.float32), 0.0)
    scaled = grad_f * (0.5 + half_tanh)
    grad_up = scaled * gate_f
    grad_gate = up_rows.astype(jnp.float32) * (scaled + grad_up * (0.5 - half_tanh))
    return grad_gate.astype(jnp.bfloat16), grad_up.astype(jnp.bfloat16)


def kernel(
    layout_ref, grad_hbm, gate_hbm, up_hbm, w_gate_hbm, w_up_hbm, out_hbm,
    stage, acts, weights,
    first, second, third, across, near, far,
    halved, joined, r_first, r_second, r_third, r_near, r_far, a_near, a_far, a_last,
    stage_sem, load_sem,
    send1, recv1, send2, recv2, send3, recv3, send4, recv4, send5, recv5, send6, recv6,
    r_send0, r_recv0, r_send1, r_recv1, r_send2, r_recv2, r_send4, r_recv4, r_send5, r_recv5, r_send6, r_recv6,
    a_send4, a_recv4, a_send5, a_recv5, a_send6, a_recv6, out_sem,
):
    section = lax.axis_index("section")
    dp = lax.axis_index("dp")
    tensor = lax.axis_index("tensor")
    y, x = dp // RING, dp % RING
    hidden = w_gate_hbm.shape[0]
    my_expert = (dp * 2 + tensor) * hidden // F

    def turned(value, by):
        return (value + by) % RING

    xs = [turned(x, by) for by in range(RING)]
    ys = [turned(y, by) for by in range(RING)]
    x_devices = [(section, y * RING + xs[by], tensor) for by in range(RING)]
    y_devices = [(section, ys[by] * RING + x, tensor) for by in range(RING)]

    outer = (xs, ys)
    inner = (ys, xs)
    outer_device = (x_devices, y_devices)
    inner_device = (y_devices, x_devices)
    partner = (section, dp, 1 - tensor)
    before = ((section + 3) % 4, dp, tensor)

    def fetch(k, kind):
        source = (grad_hbm, gate_hbm, up_hbm)[kind]
        return pltpu.make_async_copy(source.at[:, xs[k]], stage.at[k, kind], stage_sem.at[k, kind])

    def tile_of(part, c):
        return part * CHUNKS + c

    def r_tile_of(part):
        return 2 * CHUNKS + part

    def columns_of(tile):
        return pl.ds(pl.multiple_of(tile * TILE, TILE), TILE)

    def load(tile, kind):
        source = (w_gate_hbm, w_up_hbm)[kind]
        return pltpu.make_async_copy(
            source.at[:, columns_of(tile)],
            weights.at[tile, pl.ds(kind * hidden, hidden), :],
            load_sem.at[tile, kind],
        )

    def load_start(tile):
        for kind in range(2):
            load(tile, kind).start()

    def load_wait(tile):
        for kind in range(2):
            load(tile, kind).wait()

    for kind in range(3):
        fetch(2, kind).start()
    load_start(tile_of(0, 0))

    barrier = pltpu.get_barrier_semaphore()
    peers = [x_devices[1], x_devices[3], y_devices[1], y_devices[3], partner]
    peers += [((section + by) % 4, dp, half) for by in (1, 3) for half in range(2)]
    for peer in peers:
        pl.semaphore_signal(barrier, inc=1, device_id=peer, device_id_type=MESH)

    for k in (0, 1, 3):
        for kind in range(3):
            fetch(k, kind).start()
    load_start(tile_of(1, 0))

    def load_rest():
        @pl.loop(1, CHUNKS)
        def _(c):
            for part in range(2):
                load_start(tile_of(part, c))

    def make_acts(down, along):
        row, column = turned(y, down), turned(x, along)
        mine = layout_ref[0, row * RING + column] == my_expert

        @pl.loop(0, 2 * HALF // STRIP // UNROLL)
        def _(i):
            for k in range(UNROLL):
                strip = i * UNROLL + k
                half = strip // (HALF // STRIP)
                rows = pl.ds(pl.multiple_of(strip % (HALF // STRIP) * STRIP, STRIP), STRIP)
                held = [stage[along, kind, row, half, rows] for kind in range(3)]
                pair = swiglu_grads(*held, mine)
                acts[row, column, half, rows, :hidden] = pair[0]
                acts[row, column, half, rows, hidden:] = pair[1]

    def remote(src, dst, send, recv, device):
        return pltpu.make_async_remote_copy(
            src_ref=src, dst_ref=dst, send_sem=send, recv_sem=recv, device_id=device, device_id_type=MESH
        )

    def by_way(way):
        return 1 if way == 0 else 3

    def step1(part, c, way):
        return remote(
            first.at[part, c, way], second.at[part, c, way, way],
            send1.at[part, c, way], recv1.at[part, c, way], outer_device[part][by_way(way)],
        )

    def step2(part, c, way):
        return remote(
            second.at[part, c, way], third.at[part, c, way],
            send2.at[part, c, way], recv2.at[part, c, way], outer_device[part][by_way(way)],
        )

    def step3(part, c):
        return remote(
            third.at[part, c, 0, 1 - tensor], across.at[part, c], send3.at[part, c], recv3.at[part, c], partner
        )

    def step4(part, c, way):
        return remote(
            third.at[part, c, 0, tensor, inner[part][2], pl.ds(way * QUARTER, QUARTER)], near.at[part, c, way],
            send4.at[part, c, way], recv4.at[part, c, way], inner_device[part][by_way(way)],
        )

    def step5(part, c, way):
        return remote(
            third.at[part, c, 0, tensor, inner[part][by_way(way)]], far.at[part, c, way],
            send5.at[part, c, way], recv5.at[part, c, way], inner_device[part][by_way(way)],
        )

    def step6(part, c):
        return remote(
            far.at[part, c, 0], out_hbm.at[:, columns_of(tile_of(part, c))],
            send6.at[part, c], recv6.at[part, c], before,
        )

    def r_step0(part):
        return remote(halved.at[part], joined.at[part], r_send0.at[part], r_recv0.at[part], partner)

    def r_step1(part, way):
        return remote(
            r_first.at[part, pl.ds(2 * way, 2)], r_second.at[part, way, pl.ds(2 * way, 2)],
            r_send1.at[part, way], r_recv1.at[part, way], outer_device[part][by_way(way)],
        )

    def r_step2(part, way):
        return remote(
            r_second.at[part, way], r_third.at[part, way],
            r_send2.at[part, way], r_recv2.at[part, way], outer_device[part][by_way(way)],
        )

    def r_step4(part, way):
        return remote(
            r_third.at[part, 0, inner[part][2], pl.ds(way * QUARTER, QUARTER)], r_near.at[part, way],
            r_send4.at[part, way], r_recv4.at[part, way], inner_device[part][by_way(way)],
        )

    def r_step5(part, way):
        return remote(
            r_third.at[part, 0, inner[part][by_way(way)]], r_far.at[part, way],
            r_send5.at[part, way], r_recv5.at[part, way], inner_device[part][by_way(way)],
        )

    def r_step6(part):
        return remote(
            r_far.at[part, 0], out_hbm.at[:, columns_of(r_tile_of(part))],
            r_send6.at[part], r_recv6.at[part], before,
        )

    def a_step4(part, way):
        return remote(
            third.at[part, LAST, 0, way, inner[part][2]], a_near.at[part, way],
            a_send4.at[part, way], a_recv4.at[part, way], inner_device[part][by_way(way)],
        )

    def a_step5(part, way):
        return remote(
            third.at[part, LAST, 0, :, inner[part][by_way(way)]], a_far.at[part, way],
            a_send5.at[part, way], a_recv5.at[part, way], inner_device[part][by_way(way)],
        )

    def a_step6(part, half, source):
        return remote(
            third.at[part, LAST, 0, half, inner[part][0]], a_last.at[part, source],
            a_send6.at[part, half], a_recv6.at[part, source], ((section + 3) % 4, dp, half),
        )

    def a_out(part):
        return pltpu.make_async_copy(
            a_last.at[part, 0], out_hbm.at[:, columns_of(tile_of(part, LAST))], out_sem.at[part]
        )

    def dot(rows, tile):
        rows = rows.reshape(-1, 2 * hidden)
        return jnp.dot(rows, weights[tile], preferred_element_type=jnp.float32)

    def product(part, c, chunk):
        rows = acts[:, chunk] if part == 0 else acts[chunk]
        return dot(rows, tile_of(part, c)).reshape(RING, 2, HALF, TILE)

    def r_product(part, chunk):
        rows = acts[:, chunk, tensor] if part == 0 else acts[chunk, :, tensor]
        held = joined[part, :, chunk] if part == 0 else joined[part, chunk]
        return dot(rows, r_tile_of(part)).reshape(RING, HALF, TILE) + held.astype(jnp.float32)

    def phase0(c):
        for part in range(2):
            load_wait(tile_of(part, c))
            total = product(part, c, outer[part][2]).astype(jnp.bfloat16)
            for way in range(2):
                first[part, c, way] = total[:, way]
                step1(part, c, way).start()

            if part == 0:

                @pl.when(c == 0)
                def _():
                    for part in range(2):
                        load_start(r_tile_of(part))
                    for k in (0, 1, 3):
                        for kind in range(3):
                            fetch(k, kind).wait()

                    @pl.loop(0, 3)
                    def _(i):
                        make_acts(2, turned(i, 3))

        pl.when(c == 0)(load_rest)

    def phase1(c):
        for part in range(2):
            for way in range(2):
                total = product(part, c, outer[part][by_way(way)])
                step1(part, c, way).wait_recv()
                held = second[part, c, way, way].astype(jnp.float32)
                second[part, c, way, way] = (total[:, way] + held).astype(jnp.bfloat16)
                second[part, c, way, 1 - way] = total[:, 1 - way].astype(jnp.bfloat16)
                step2(part, c, way).start()

    def phase2(c):
        for part in range(2):
            total = product(part, c, outer[part][0])
            for way in range(2):
                step2(part, c, way).wait_recv()
            for half in range(2):
                held = third[part, c, 0, half].astype(jnp.float32) + third[part, c, 1, half].astype(jnp.float32)
                third[part, c, 0, half] = (total[:, half] + held).astype(jnp.bfloat16)

            @pl.when(c < LAST)
            def _():
                step3(part, c).start()

            @pl.when(c == LAST)
            def _():
                for way in range(2):
                    a_step4(part, way).start()

    def phase3(c):
        for part in range(2):
            step3(part, c).wait_recv()
            total = third[part, c, 0, tensor].astype(jnp.float32) + across[part, c].astype(jnp.float32)
            third[part, c, 0, tensor] = total.astype(jnp.bfloat16)
            for way in range(2):
                step4(part, c, way).start()

    def phase4(c):
        for part in range(2):
            for way in range(2):
                step4(part, c, way).wait_recv()
                spot = inner[part][by_way(way)]
                rows = pl.ds(way * QUARTER, QUARTER)
                total = third[part, c, 0, tensor, spot, rows].astype(jnp.float32)
                total += near[part, c, way].astype(jnp.float32)
                third[part, c, 0, tensor, spot, rows] = total.astype(jnp.bfloat16)
                step5(part, c, way).start()

    def phase5(c):
        for part in range(2):
            for way in range(2):
                step5(part, c, way).wait_recv()
            total = third[part, c, 0, tensor, inner[part][0]].astype(jnp.float32)
            total += far[part, c, 0].astype(jnp.float32)
            total += far[part, c, 1].astype(jnp.float32)
            far[part, c, 0] = total.astype(jnp.bfloat16)
            step6(part, c).start()

    def r_phase0():
        @pl.loop(0, 9)
        def _(i):
            make_acts(turned(i // 3, 3), turned(i % 3, 3))

        for part in range(2):
            load_wait(r_tile_of(part))
            for k in range(2):
                total = dot(acts[2 * k : 2 * k + 2, :, 1 - tensor], r_tile_of(part)).astype(jnp.bfloat16)
                halved[part, 2 * k : 2 * k + 2] = total.reshape(2, RING, HALF, TILE)
            r_step0(part).start()

    def r_phase1():
        for part in range(2):
            r_step0(part).wait_recv()
            r_first[part] = r_product(part, outer[part][2]).astype(jnp.bfloat16)
            for way in range(2):
                r_step1(part, way).start()

    def r_phase2():
        for part in range(2):
            for way in range(2):
                total = r_product(part, outer[part][by_way(way)])
                r_step1(part, way).wait_recv()
                here, there = 2 * way, 2 * (1 - way)
                held = r_second[part, way, here : here + 2].astype(jnp.float32)
                r_second[part, way, here : here + 2] = (total[here : here + 2] + held).astype(jnp.bfloat16)
                r_second[part, way, there : there + 2] = total[there : there + 2].astype(jnp.bfloat16)
                r_step2(part, way).start()

    def r_phase3():
        for part in range(2):
            total = r_product(part, outer[part][0])
            for way in range(2):
                r_step2(part, way).wait_recv()
            total += r_third[part, 0].astype(jnp.float32)
            total += r_third[part, 1].astype(jnp.float32)
            r_third[part, 0] = total.astype(jnp.bfloat16)
            for way in range(2):
                r_step4(part, way).start()

    def r_phase4():
        for part in range(2):
            for way in range(2):
                r_step4(part, way).wait_recv()
                spot = inner[part][by_way(way)]
                rows = pl.ds(way * QUARTER, QUARTER)
                total = r_third[part, 0, spot, rows].astype(jnp.float32)
                total += r_near[part, way].astype(jnp.float32)
                r_third[part, 0, spot, rows] = total.astype(jnp.bfloat16)
                r_step5(part, way).start()

    def r_phase5():
        for part in range(2):
            for way in range(2):
                r_step5(part, way).wait_recv()
            total = r_third[part, 0, inner[part][0]].astype(jnp.float32)
            total += r_far[part, 0].astype(jnp.float32)
            total += r_far[part, 1].astype(jnp.float32)
            r_far[part, 0] = total.astype(jnp.bfloat16)
            r_step6(part).start()

    def a_phase3():
        for part in range(2):
            for way in range(2):
                a_step4(part, way).wait_recv()
                spot = inner[part][by_way(way)]
                total = third[part, LAST, 0, way, spot].astype(jnp.float32) + a_near[part, way].astype(jnp.float32)
                third[part, LAST, 0, way, spot] = total.astype(jnp.bfloat16)
                a_step5(part, way).start()

    def a_phase4():
        for part in range(2):
            for way in range(2):
                a_step5(part, way).wait_recv()
            for half in range(2):
                total = third[part, LAST, 0, half, inner[part][0]].astype(jnp.float32)
                total += a_far[part, 0, half].astype(jnp.float32)
                total += a_far[part, 1, half].astype(jnp.float32)
                third[part, LAST, 0, half, inner[part][0]] = total.astype(jnp.bfloat16)
                a_step6(part, half, tensor).start()

    def a_phase5():
        for part in range(2):
            for source in range(2):
                a_step6(part, 0, source).wait_recv()
            total = a_last[part, 0].astype(jnp.float32) + a_last[part, 1].astype(jnp.float32)
            a_last[part, 0] = total.astype(jnp.bfloat16)
            a_out(part).start()

    for kind in range(3):
        fetch(2, kind).wait()

    @pl.loop(0, RING)
    def _(i):
        make_acts(i, 2)

    pl.semaphore_wait(barrier, len(peers))

    phases = (phase0, phase1, phase2, phase3, phase4, phase5)
    r_phases = (r_phase0, r_phase1, r_phase2, r_phase3, r_phase4, r_phase5)
    a_phases = (a_phase3, a_phase4, a_phase5)

    @pl.loop(0, max(LAST + LAGS[-1], R_LAGS[-1] + 1, A_LAGS[-1] + 1))
    def _(slot):
        for i in range(6):
            count = CHUNKS if i < 3 else LAST

            @pl.when((slot >= LAGS[i]) & (slot < count + LAGS[i]))
            def _():
                phases[i](slot - LAGS[i])

            if i >= 3:
                pl.when(slot == A_LAGS[i - 3])(a_phases[i - 3])

            pl.when(slot == R_LAGS[i])(r_phases[i])

    @pl.loop(0, CHUNKS)
    def _(c):
        for part in range(2):
            for way in range(2):
                for step in (step1, step2):
                    step(part, c, way).wait_send()

    @pl.loop(0, LAST)
    def _(c):
        for part in range(2):
            step6(part, c).wait()
            step3(part, c).wait_send()
            for way in range(2):
                for step in (step4, step5):
                    step(part, c, way).wait_send()

    for part in range(2):
        a_out(part).wait()
        r_step6(part).wait()
        r_step0(part).wait_send()
        for way in range(2):
            for step in (r_step1, r_step2, r_step4, r_step5, a_step4, a_step5):
                step(part, way).wait_send()
            a_step6(part, way, tensor).wait_send()


def per_device(grad_hidden, gate_pre, up_pre, w_gate, w_up, block_expert):
    hidden, model = w_gate.shape[1:]
    rows = grad_hidden.shape[1]
    blocked = (RING, RING, 2, HALF, hidden)
    dma = pltpu.SemaphoreType.DMA
    anywhere = pl.BlockSpec(memory_space=pl.ANY)

    def room(*shape):
        return pltpu.VMEM(shape, jnp.bfloat16)

    both, single = dma((2, CHUNKS, 2)), dma((2, CHUNKS))
    pairs, two = dma((2, 2)), dma((2,))
    out = pl.pallas_call(
        kernel,
        out_shape=jax.ShapeDtypeStruct((HALF, model), jnp.bfloat16),
        in_specs=[pl.BlockSpec(memory_space=pltpu.SMEM)] + [anywhere] * 5,
        out_specs=anywhere,
        scratch_shapes=[
            room(RING, 3, RING, 2, HALF, hidden),
            room(RING, RING, 2, HALF, 2 * hidden),
            room(model // TILE, 2 * hidden, TILE),
            room(2, CHUNKS, 2, RING, HALF, TILE),
            room(2, CHUNKS, 2, 2, RING, HALF, TILE),
            room(2, CHUNKS, 2, 2, RING, HALF, TILE),
            room(2, LAST, RING, HALF, TILE),
            room(2, LAST, 2, QUARTER, TILE),
            room(2, LAST, 2, HALF, TILE),
            room(2, RING, RING, HALF, TILE),
            room(2, RING, RING, HALF, TILE),
            room(2, RING, HALF, TILE),
            room(2, 2, RING, HALF, TILE),
            room(2, 2, RING, HALF, TILE),
            room(2, 2, QUARTER, TILE),
            room(2, 2, HALF, TILE),
            room(2, 2, HALF, TILE),
            room(2, 2, 2, HALF, TILE),
            room(2, 2, HALF, TILE),
            dma((RING, 3)),
            dma((model // TILE, 2)),
        ]
        + [both] * 4
        + [single] * 2
        + [both] * 4
        + [single] * 2
        + [two] * 2
        + [pairs] * 8
        + [two] * 2
        + [pairs] * 6
        + [two],
        cost_estimate=pl.CostEstimate(
            flops=4 * rows * hidden * model, bytes_accessed=6 * hidden * rows + 4 * hidden * model, transcendentals=0
        ),
        compiler_params=pltpu.CompilerParams(
            collective_id=0, has_side_effects=True, vmem_limit_bytes=61 * 1024 * 1024
        ),
    )(
        block_expert,
        grad_hidden.reshape(blocked),
        gate_pre.reshape(blocked),
        up_pre.reshape(blocked),
        w_gate[0],
        w_up[0],
    )
    return out[None]


def solution(mesh):
    return jax.shard_map(
        per_device,
        mesh=mesh,
        in_specs=(
            P("section", None, ("dp", "tensor")),
            P("section", None, ("dp", "tensor")),
            P("section", None, ("dp", "tensor")),
            P("section", ("dp", "tensor"), None),
            P("section", ("dp", "tensor"), None),
            P("section", None),
        ),
        out_specs=P("section", ("dp", "tensor"), None),
        check_vma=False,
    )
```
